256 devices in a mesh: dp: 2 (over core), ctx: 128 (over z, y, x).
Axes of the slice: x: 4, y: 4, z: 8, core: 2. Of those that a mesh axis runs over, the one named last changes fastest.
Arguments:
- hidden: bfloat16 [4, 16384, 5376], P('dp', 'ctx'), parts along dimension 0, may hold values from -400 to 400
- queries: bfloat16 [4, 16384, 2048], P('dp', 'ctx'), parts along dimension 0, may hold values from -400 to 400
- input_gain: float32 [5376], replicated, may hold values from 0.1 to 1.9
- kv_weight: bfloat16 [5376, 2048], P('ctx'), may hold values from -0.078125 to 0.078125
- query_gain: float32 [128], replicated, may hold values from 1 to 2.5
- key_gain: float32 [128], replicated, may hold values from 1 to 2.5
Outputs:
- attended: bfloat16 [4, 16384, 2048], P('dp', 'ctx'), parts along dimension 0
The draws below stay inside these ranges and needn't reach their ends.
There are 2 independent parts, one for each index of `dp`. The reference program is written for one: setup_inputs(seed, part) draws one part's arguments, and reference() takes and returns one part's arrays. A program takes and returns all parts, laid end to end along the dimension named above; an argument that names none is the same for every part. Nothing has to cross between parts.
All inputs are finite; a program needn't handle non-finite values.
Results may differ from the reference program's by a relative error of at most 0.012.
Values may be sent and summed in bfloat16 or wider, within the bound.
A program may use at most 128 MiB of HBM per device.

```python
import math
import jax
import jax.numpy as jnp
from jax import lax

D = 5376
QH = 16
KVH = 8
HD = 128
WINDOW = 1024
TOK_DEV = 128
SEQS = 2
LENGTH = 16384


def scaled_field(key, field_shape):
    base_key, row_key, column_key = jax.random.split(key, 3)
    row_shape = field_shape[:-1] + (1,)
    base_values = jax.random.truncated_normal(base_key, -4.0, 4.0, field_shape, jnp.float32)
    row_scale = jnp.exp(jax.random.uniform(row_key, row_shape, jnp.float32, 0.0, math.log(10.0)))
    column_scale = jnp.exp(jax.random.uniform(column_key, (field_shape[-1],), jnp.float32, 0.0, math.log(10.0)))
    return (base_values * row_scale * column_scale).astype(jnp.bfloat16)


def draw_hidden(key, part):
    return scaled_field(jax.random.fold_in(key, 11), (SEQS, LENGTH, D))


def draw_queries(key, part):
    return scaled_field(jax.random.fold_in(key, 23), (SEQS, LENGTH, QH * HD))


def steps_of(rng, shape, pieces, low, largest):
    def one(dim, shards_of):
        heights = jax.random.uniform(jax.random.fold_in(jax.random.fold_in(rng, 6), dim), (shards_of,), jnp.float32, low / len(pieces), largest / len(pieces))
        return jnp.repeat(jnp.exp(heights), shape[dim] // shards_of).reshape((-1,) + (1,) * (len(shape) - dim - 1))

    factor_of = one(*pieces[0])
    for cut in pieces[1:]:
        factor_of = factor_of * one(*cut)
    return factor_of


def normal_values(own_key, extent, scale, limit, pieces=(), held_as=jnp.bfloat16):
    entries = jax.random.normal(own_key, extent, jnp.float32) * scale
    if len(pieces) > 0:
        entries = steps_of(own_key, extent, pieces, -0.22, 0.18) * entries
    return jnp.clip(entries, min=-limit, max=limit).astype(held_as)


def setup_inputs(seed: int = 0, part: int = 0) -> dict:
    splits = jax.random.split(jax.random.key(seed), 7)
    part_keys = jax.random.split(jax.random.fold_in(splits[6], part), 7)
    hidden = draw_hidden(jax.random.fold_in(jax.random.fold_in(splits[6], part), 71), part)
    queries = draw_queries(jax.random.fold_in(jax.random.fold_in(splits[6], part), 71), part)
    input_gain = jnp.clip(1.0 + 0.18 * jax.random.normal(splits[2], (D,), jnp.float32), 0.1, 1.9)
    kv_weight = normal_values(splits[3], (D, 2 * KVH * HD), D ** -0.5, 0.078125, ((0, 128),))
    query_gain = jnp.clip(jnp.exp(jax.random.uniform(splits[4], (HD,), jnp.float32, math.log(1.0), math.log(2.5))), 1.0, 2.5)
    key_gain = jnp.clip(jnp.exp(jax.random.uniform(splits[5], (HD,), jnp.float32, math.log(1.0), math.log(2.5))), 1.0, 2.5)
    return dict(hidden=hidden, queries=queries, input_gain=input_gain, kv_weight=kv_weight, query_gain=query_gain, key_gain=key_gain)


attn_scalar = 168.0
norm_eps = 1e-06

def rotary_tables(positions, head_width):
    half_width = head_width // 2
    exponent = 2.0 * jnp.arange(half_width, dtype=jnp.float32) / head_width
    inverse = jnp.power(10000.0, -exponent)
    angles = positions.astype(jnp.float32)[:, None] * inverse[None, :]
    return (jnp.cos(angles), jnp.sin(angles))

def rotate(heads, cos_table, sine_table):
    half_width = heads.shape[-1] // 2
    first = heads[..., :half_width]
    second = heads[..., half_width:]
    cos_part = cos_table[:, None, :]
    sine_part = sine_table[:, None, :]
    return jnp.concatenate([first * cos_part - second * sine_part, second * cos_part + first * sine_part], axis=-1)

def head_norm(heads, gain):
    return heads * lax.rsqrt(lax.optimization_barrier(jnp.mean(heads * heads, axis=-1, keepdims=True)) + norm_eps) * gain

def reference(hidden, queries, input_gain, kv_weight, query_gain, key_gain):
    kv_half = KVH * HD
    group_size = QH // KVH
    results = []
    for seq_index in range(SEQS):
        hidden_f32 = hidden[seq_index].astype(jnp.float32)
        normed = (hidden_f32 * lax.rsqrt(lax.optimization_barrier(jnp.mean(hidden_f32 * hidden_f32, axis=-1, keepdims=True)) + norm_eps) * input_gain).astype(jnp.bfloat16)
        projected = jnp.dot(normed, kv_weight, preferred_element_type=jnp.float32)
        positions = jnp.arange(LENGTH, dtype=jnp.int32)
        cos_table, sine_table = rotary_tables(positions, HD)
        key_rows = rotate(head_norm(projected[:, :kv_half].reshape(LENGTH, KVH, HD), key_gain), cos_table, sine_table)
        key_rows = lax.optimization_barrier(key_rows.astype(jnp.bfloat16))
        value_rows = lax.optimization_barrier(projected[:, kv_half:].reshape(LENGTH, KVH, HD).astype(jnp.bfloat16))
        query_f32 = queries[seq_index].astype(jnp.float32).reshape(LENGTH, QH, HD)
        query_rows = rotate(head_norm(query_f32, query_gain), cos_table, sine_table) * attn_scalar ** (-0.5)
        query_rows = lax.optimization_barrier(query_rows.astype(jnp.bfloat16))
        padded_keys = jnp.pad(key_rows, ((WINDOW, 0), (0, 0), (0, 0)))
        padded_values = jnp.pad(value_rows, ((WINDOW, 0), (0, 0), (0, 0)))

        def one_block(block_index):
            row_start = (block_index * TOK_DEV).astype(jnp.int32)
            query_block = lax.dynamic_slice_in_dim(query_rows, row_start, TOK_DEV, 0).reshape(TOK_DEV, KVH, group_size, HD)
            near_keys = lax.dynamic_slice_in_dim(padded_keys, row_start, WINDOW + TOK_DEV, 0)
            near_values = lax.dynamic_slice_in_dim(padded_values, row_start, WINDOW + TOK_DEV, 0)
            query_pos = row_start + jnp.arange(TOK_DEV, dtype=jnp.int32)
            key_pos = row_start - WINDOW + jnp.arange(WINDOW + TOK_DEV, dtype=jnp.int32)
            allowed = (key_pos[None, :] <= query_pos[:, None]) & (key_pos[None, :] > query_pos[:, None] - WINDOW) & (key_pos[None, :] >= 0)
            scores = jnp.einsum('qhgd,khd->hgqk', query_block.astype(jnp.float32), near_keys.astype(jnp.float32))
            weights = jnp.where(allowed, jnp.exp(scores), 0.0)
            row_total = lax.optimization_barrier(jnp.sum(weights, axis=-1))
            rounded = lax.optimization_barrier(weights.astype(jnp.bfloat16)).astype(jnp.float32)
            weighted = jnp.einsum('hgqk,khd->qhgd', rounded, near_values.astype(jnp.float32))
            result = weighted / jnp.transpose(row_total, (2, 0, 1))[..., None]
            return result.astype(jnp.bfloat16).reshape(TOK_DEV, QH * HD)
        blocks = lax.map(one_block, jnp.arange(LENGTH // TOK_DEV, dtype=jnp.int32))
        results.append(blocks.reshape(LENGTH, QH * HD))
    return jnp.stack(results, axis=0)
```

```python
import jax
import jax.numpy as jnp
from jax import lax
from jax.experimental import pallas as pl
from jax.experimental.pallas import tpu as pltpu
from jax.sharding import PartitionSpec as P

HD = 128
WINDOW = 1024
EPS = 1e-6
SCALE = 168.0 ** -0.5
NX, NY, NZ = 4, 4, 8
PLANE = NX * NY
SLABS = WINDOW // HD
MEMBERS = 8
ROWS_B, ROWS_C = 176, 160
BF = jnp.bfloat16
F32 = jnp.float32
MESH = pl.DeviceIdType.MESH


def head_rotary(head, gain, cos, sin):
    mean = jnp.mean(head * head, axis=-1, keepdims=True)
    unit = head * lax.rsqrt(mean + EPS) * gain
    return unit * cos + pltpu.roll(unit, 64, 1) * sin


def kernel(
    w_ref, h_ref, q_ref, gain_ref, qg_ref, kg_ref, cos_ref, sin_ref, o_ref,
    landing, wb, wc, xn, acc, kvs, kvb, qn, qb, ob,
    a_s, a_r, row_s, row_r, z_s, z_r, l_s, l_r, x_s, x_r,
    q_s, q_r, kv_s, kv_r, halo_s, o_s, o_r,
):
    c = lax.axis_index("dp")
    t = lax.axis_index("ctx")
    z = lax.div(t, PLANE)
    i = lax.rem(t, PLANE)
    y = lax.div(i, NX)
    x = lax.rem(i, NX)
    yh = lax.div(y, 2)
    yl = lax.rem(y, 2)
    block_len = cos_ref.shape[0]

    def chip(zz, yy, xx):
        return zz * PLANE + yy * NX + xx

    def step(v, d, n):
        return lax.rem(v + (d % n), n)

    sibling = (1 - c, t)
    pending = []

    def remote(src, dst, send, recv, device):
        return pltpu.make_async_remote_copy(
            src_ref=src, dst_ref=dst, send_sem=send, recv_sem=recv,
            device_id=device, device_id_type=MESH,
        )

    def push(src, dst, send, recv, device):
        copy = remote(src, dst, send, recv, device)
        copy.start()
        pending.append(copy)

    def arrived(region, recv):
        pltpu.make_async_copy(region, region, recv).wait()

    barrier = pltpu.get_barrier_semaphore()
    for r in range(1, 2 * PLANE):
        dev = (lax.rem(c + r % 2, 2), z * PLANE + lax.rem(i + r // 2, PLANE))
        pl.semaphore_signal(barrier, inc=1, device_id=dev, device_id_type=MESH)
    for d in (1, -1):
        pl.semaphore_signal(
            barrier, inc=1, device_id=(c, chip(step(z, d, NZ), y, x)), device_id_type=MESH
        )

    cos = cos_ref[...]
    sin = sin_ref[...]
    qg = qg_ref[...]
    kg = kg_ref[...]
    for s in range(2):
        for h in range(16):
            head = q_ref[s, :, h * HD:(h + 1) * HD].astype(F32)
            qn[s, :, h * HD:(h + 1) * HD] = (head_rotary(head, qg, cos, sin) * SCALE).astype(BF)

    pl.semaphore_wait(barrier, 2 * PLANE - 1 + 2)

    j = yl * NX + x
    for r in range(1, MEMBERS):
        peer = lax.rem(j + r, MEMBERS)
        pyl, px = lax.div(peer, NX), lax.rem(peer, NX)
        col = pl.multiple_of(pyl * 1024 + c * 512 + px * HD, HD)
        push(
            w_ref.at[:, pl.ds(col, HD)], landing.at[j], a_s.at[r], a_r.at[r],
            (c, chip(z, yh * 2 + pyl, px)),
        )
    col = pl.multiple_of(yl * 1024 + c * 512 + x * HD, HD)
    landing[j] = w_ref[:, pl.ds(col, HD)]

    def q_pieces(start):
        for k in range(8):
            for kk in range(2):
                low = lax.rem(i + k, 8)
                core = lax.rem(c + kk, 2)
                s = lax.div(low, 4)
                h = core * 4 + lax.rem(low, 4)
                src = qn.at[s, :, pl.ds(pl.multiple_of(h * 256, 256), 256)]
                dst = qb.at[i]
                dev = (core, z * PLANE + c * 8 + low)
                send, recv = q_s.at[k * 2 + kk], q_r.at[i]
                if k == 0 and kk == 0:
                    here = lax.div(i, 8) == c

                    @pl.when(here)
                    def _():
                        if start:
                            pltpu.make_async_copy(src, dst, recv).start()

                    @pl.when(jnp.logical_not(here))
                    def _():
                        copy = remote(src, dst, send, recv, dev)
                        copy.start() if start else copy.wait_send()
                else:
                    copy = remote(src, dst, send, recv, dev)
                    copy.start() if start else copy.wait_send()

    for r in range(1, MEMBERS):
        arrived(landing.at[lax.rem(j + MEMBERS - r, MEMBERS)], a_r.at[r])
    rows = jnp.concatenate([landing[m].astype(F32) for m in range(MEMBERS)], axis=0).astype(BF)
    wb[y, z, x] = rows[:ROWS_B]
    wc[x, z, y] = rows[ROWS_B:]

    for d in (1, 3, 2):
        push(wb.at[y, z, x], wb.at[y, z, x], row_s.at[d], row_r.at[d], (c, chip(z, y, step(x, d, NX))))
        push(wc.at[x, z, y], wc.at[x, z, y], row_s.at[4 + d], row_r.at[4 + d], (c, chip(z, step(y, d, NY), x)))
    for d in (1, 3, 2):
        arrived(wb.at[y, z, step(x, -d, NX)], row_r.at[d])
        arrived(wc.at[x, z, step(y, -d, NY)], row_r.at[4 + d])

    def chunk(part, line, zz):
        return wb.at[line, zz] if part == 0 else wc.at[line, zz]

    def half(part, line, zz, which):
        ref = wb if part == 0 else wc
        return ref.at[line, zz, pl.ds(2 * which, 2)]

    def line_device(part, d):
        if part == 0:
            return (c, chip(z, step(y, d, NY), x))
        return (c, chip(z, y, step(x, d, NX)))

    own = (y, x)
    along = (NY, NX)

    def z_sem(part, way, d):
        return (part * 2 + way) * 5 + d

    def l_sem(part, way, kind, slot):
        return ((part * 2 + way) * 2 + kind) * 8 + slot

    def z_send(part, zz, way, d):
        dev = (c, chip(step(z, 1 if way == 0 else -1, NZ), y, x))
        ref = chunk(part, own[part], zz) if d < 4 else half(part, own[part], zz, way)
        n = z_sem(part, way, d)
        push(ref, ref, z_s.at[n], z_r.at[n], dev)

    def z_wait(part, zz, way, d):
        ref = chunk(part, own[part], zz) if d < 4 else half(part, own[part], zz, way)
        arrived(ref, z_r.at[z_sem(part, way, d)])

    def line_send(part, zz, slot):
        for way, d in ((0, 1), (1, -1)):
            ref = chunk(part, own[part], zz)
            n = l_sem(part, way, 0, slot)
            push(ref, ref, l_s.at[n], l_r.at[n], line_device(part, d))

    def line_relay(part, zz, slot):
        for way, d in ((0, 1), (1, -1)):
            line = step(own[part], -d, along[part])
            arrived(chunk(part, line, zz), l_r.at[l_sem(part, way, 0, slot)])
            ref = half(part, line, zz, way)
            n = l_sem(part, way, 1, slot)
            push(ref, ref, l_s.at[n], l_r.at[n], line_device(part, d))

    def line_finish(part, zz, slot):
        for way in range(2):
            line = step(own[part], 2, along[part])
            arrived(half(part, line, zz, way), l_r.at[l_sem(part, way, 1, slot)])

    def slots(k):
        if k == 0:
            return [(z, 0)]
        if k == 4:
            return [(step(z, 4, NZ), 7)]
        return [(step(z, -k, NZ), k), (step(z, k, NZ), 3 + k)]

    def norm_rows(first, count):
        def one(n, carry):
            at = pl.multiple_of(first + n * 16, 16)
            s, row = lax.div(at, block_len), pl.multiple_of(lax.rem(at, block_len), 16)
            v = h_ref[s, pl.ds(row, 16), :].astype(F32)
            mean = jnp.mean(v * v, axis=-1, keepdims=True)
            xn[c, pl.ds(at, 16), :] = (v * lax.rsqrt(mean + EPS) * gain_ref[...]).astype(BF)
            return carry

        lax.fori_loop(0, count // 16, one, 0)

    for k in range(5):
        if k > 0:
            for way, (zz, _) in enumerate(slots(k) if k < 4 else slots(k) * 2):
                for part in range(2):
                    z_wait(part, zz, way, k)
                    if k < 4:
                        z_send(part, zz, way, k + 1)
        else:
            for way in range(2):
                for part in range(2):
                    z_send(part, z, way, 1)
        for zz, slot in slots(k):
            for part in range(2):
                line_send(part, zz, slot)
        if k == 0:
            q_pieces(True)
            norm_rows(0, 2 * block_len)
            push(xn.at[c], xn.at[c], x_s, x_r, sibling)
        if k > 0:
            for zz, slot in slots(k - 1):
                for part in range(2):
                    line_relay(part, zz, slot)
    for zz, slot in slots(4):
        for part in range(2):
            line_relay(part, zz, slot)
    for k in range(5):
        for zz, slot in slots(k):
            for part in range(2):
                line_finish(part, zz, slot)
    arrived(xn.at[1 - c], x_r)

    def project(n):
        nyl, nx = n // 2, 2 * (n % 2)
        for part_z in range(2):
            pieces = []
            for zz in range(4 * part_z, 4 * part_z + 4):
                for hi in range(2):
                    ny = 2 * hi + nyl
                    pieces.append(jnp.concatenate([wb[ny, zz, nx], wb[ny, zz, nx + 1]], axis=1))
                    pieces.append(jnp.concatenate([wc[nx, zz, ny], wc[nx + 1, zz, ny]], axis=1))
            right = jnp.concatenate(pieces, axis=0)
            depth = right.shape[0]
            for g in range(2):
                left = xn[g, :, part_z * depth:(part_z + 1) * depth]
                term = jnp.dot(left, right, preferred_element_type=F32)
                if part_z == 0:
                    acc[g] = term
                else:
                    acc[g] = acc[g] + term

    def kv_pieces(e, start):
        for k in range(8):
            q = lax.rem(i + k, 8)
            u = lax.div(q, 4) * 8 + lax.rem(lax.div(q, 2), 2) * 4 + 2 * e + lax.rem(q, 2)
            src, dst = kvs.at[u], kvb.at[SLABS + i]
            send, recv = kv_s.at[e * 8 + k], kv_r.at[SLABS + i]
            here = u == i

            @pl.when(here)
            def _():
                if start:
                    pltpu.make_async_copy(src, dst, recv).start()

            @pl.when(jnp.logical_not(here))
            def _():
                copy = remote(src, dst, send, recv, (c, z * PLANE + u))
                copy.start() if start else copy.wait_send()

    for e in range(2):
        project(e)
        for g in range(2):
            for s in range(2):
                for b in range(2):
                    head = acc[g, s * block_len:(s + 1) * block_len, b * HD:(b + 1) * HD]
                    kvs[g * 8 + s * 4 + 2 * e + b, :, :HD] = head_rotary(head, kg, cos, sin).astype(BF)
        project(2 + e)
        for g in range(2):
            for s in range(2):
                for b in range(2):
                    head = acc[g, s * block_len:(s + 1) * block_len, b * HD:(b + 1) * HD]
                    kvs[g * 8 + s * 4 + 2 * e + b, :, HD:] = head.astype(BF)
        kv_pieces(e, True)

    for n in range(SLABS):
        arrived(kvb.at[16 + n], kv_r.at[16 + n])

        @pl.when(z < NZ - 1)
        def _(n=n):
            remote(
                kvb.at[16 + n], kvb.at[n], halo_s.at[n], kv_r.at[n], (c, t + PLANE)
            ).start()
    for n in range(SLABS):
        arrived(kvb.at[8 + n], kv_r.at[8 + n])
    for n in range(PLANE):
        arrived(qb.at[n], q_r.at[n])

    unit_g = lax.div(i, 8)
    unit_s = lax.rem(lax.div(i, 4), 2)
    unit_h = c * 4 + lax.rem(i, 4)
    out_col = pl.multiple_of(unit_h * 256, 256)
    row_at = lax.broadcasted_iota(jnp.int32, (2 * HD, HD), 0)
    row_at = jnp.where(row_at >= HD, row_at - HD, row_at)
    col_at = lax.broadcasted_iota(jnp.int32, (2 * HD, HD), 1)

    def out_copy(slab):
        return remote(
            ob.at[slab], o_ref.at[unit_s, :, pl.ds(out_col, 256)],
            o_s.at[slab], o_r.at[unit_s * 8 + unit_h], (unit_g, z * PLANE + slab),
        )

    def attend(slab, first_half):
        q = jnp.concatenate([qb[slab, :, :HD], qb[slab, :, HD:]], axis=0)
        total = jnp.zeros((2 * HD, 1), F32)
        out = jnp.zeros((2 * HD, HD), F32)
        for b in range(9):
            keys = kvb[slab + b, :, :HD]
            values = kvb[slab + b, :, HD:]
            scores = lax.dot_general(q, keys, (((1,), (1,)), ((), ())), preferred_element_type=F32)
            weight = jnp.exp(scores)
            if b == 0:
                weight = jnp.where(col_at > row_at, weight, 0.0)
            if b == 8:
                weight = jnp.where(col_at <= row_at, weight, 0.0)
            elif first_half:
                seen = jnp.logical_or(z > 0, slab + b >= SLABS)
                weight = jnp.where(seen, weight, 0.0)
            total = total + jnp.sum(weight, axis=-1, keepdims=True)
            out = out + jnp.dot(weight.astype(BF), values, preferred_element_type=F32)
        out = (out / total).astype(BF)
        ob[slab] = jnp.concatenate([out[:HD], out[HD:]], axis=1)
        here = jnp.logical_and(unit_g == c, slab == i)

        @pl.when(here)
        def _():
            pltpu.make_async_copy(
                ob.at[slab], o_ref.at[unit_s, :, pl.ds(out_col, 256)], o_r.at[unit_s * 8 + unit_h]
            ).start()

        @pl.when(jnp.logical_not(here))
        def _():
            out_copy(slab).start()

    def late(n, carry):
        attend(8 + lax.rem(i + n, 8), False)
        return carry

    lax.fori_loop(0, 8, late, 0)

    for n in range(SLABS):
        @pl.when(z > 0)
        def _(n=n):
            arrived(kvb.at[n], kv_r.at[n])

        @pl.when(z == 0)
        def _(n=n):
            kvb[n] = jnp.zeros((HD, 2 * HD), BF)

    def early(n, carry):
        attend(lax.rem(i + n, 8), True)
        return carry

    lax.fori_loop(0, 8, early, 0)

    for s in range(2):
        for h in range(8):
            arrived(o_ref.at[s, :, pl.ds(h * 256, 256)], o_r.at[s * 8 + h])

    for copy in pending:
        copy.wait_send()
    q_pieces(False)
    kv_pieces(0, False)
    kv_pieces(1, False)
    for n in range(SLABS):
        @pl.when(z < NZ - 1)
        def _(n=n):
            remote(
                kvb.at[16 + n], kvb.at[n], halo_s.at[n], kv_r.at[n], (c, t + PLANE)
            ).wait_send()
    for slab in range(PLANE):
        @pl.when(jnp.logical_not(jnp.logical_and(unit_g == c, slab == i)))
        def _(slab=slab):
            out_copy(slab).wait_send()


def body(hidden, queries, input_gain, kv_weight, query_gain, key_gain):
    block_len = hidden.shape[1]
    model_width = hidden.shape[2]
    positions = lax.axis_index("ctx") * block_len + jnp.arange(block_len, dtype=jnp.int32)
    exponent = 2.0 * jnp.arange(HD // 2, dtype=F32) / HD
    inverse = jnp.power(10000.0, -exponent)
    angles = positions.astype(F32)[:, None] * inverse[None, :]
    cos, sin = jnp.cos(angles), jnp.sin(angles)
    cos = jnp.concatenate([cos, cos], axis=1)
    sin = jnp.concatenate([-sin, sin], axis=1)
    dma = pltpu.SemaphoreType.DMA
    return pl.pallas_call(
        kernel,
        out_shape=jax.ShapeDtypeStruct(queries.shape, BF),
        in_specs=[pl.BlockSpec(memory_space=pltpu.VMEM)] * 8,
        out_specs=pl.BlockSpec(memory_space=pltpu.VMEM),
        scratch_shapes=[
            pltpu.VMEM((MEMBERS, 42, HD), BF),
            pltpu.VMEM((NY, NZ, NX, ROWS_B, HD), BF),
            pltpu.VMEM((NX, NZ, NY, ROWS_C, HD), BF),
            pltpu.VMEM((2, 2 * block_len, model_width), BF),
            pltpu.VMEM((2, 2 * block_len, 256), F32),
            pltpu.VMEM((16, HD, 256), BF),
            pltpu.VMEM((24, HD, 256), BF),
            pltpu.VMEM(queries.shape, BF),
            pltpu.VMEM((16, HD, 256), BF),
            pltpu.VMEM((16, HD, 256), BF),
            dma((8,)), dma((8,)), dma((8,)), dma((8,)), dma((20,)), dma((20,)),
            dma((64,)), dma((64,)), dma, dma,
            dma((16,)), dma((16,)), dma((16,)), dma((24,)), dma((8,)), dma((16,)), dma((16,)),
        ],
        compiler_params=pltpu.CompilerParams(
            collective_id=0, has_side_effects=True, vmem_limit_bytes=60 << 20
        ),
    )(
        kv_weight, hidden, queries, input_gain.reshape(1, -1),
        query_gain.reshape(1, -1), key_gain.reshape(1, -1), cos, sin,
    )


def solution(mesh):
    return jax.shard_map(
        body,
        mesh=mesh,
        in_specs=(P("dp", "ctx", None), P("dp", "ctx", None), P(), P("ctx", None), P(), P()),
        out_specs=P("dp", "ctx", None),
        check_vma=False,
    )
```

```python
import jax
import jax.numpy as jnp
from jax import lax
from jax.experimental import pallas as pl
from jax.experimental.pallas import tpu as pltpu
from jax.sharding import PartitionSpec as P

HD = 128
WINDOW = 1024
EPS = 1e-6
SCALE = 168.0 ** -0.5
NX, NY, NZ = 4, 4, 8
PLANE = NX * NY
SLABS = WINDOW // HD
MEMBERS = 8
ROWS_A, ROWS_B, ROWS_C = 80, 128, 128
PLANE_ROWS = 2 * (ROWS_A + ROWS_B + ROWS_C)
PLANE_LANES = 768
BF = jnp.bfloat16
F32 = jnp.float32
MESH = pl.DeviceIdType.MESH


def head_rotary(head, gain, cos, sin):
    mean = jnp.mean(head * head, axis=-1, keepdims=True)
    unit = head * lax.rsqrt(mean + EPS) * gain
    return unit * cos + pltpu.roll(unit, 64, 1) * sin


def kernel(
    w_hbm, h_hbm, q_hbm, gain_hbm, qg_hbm, kg_hbm, cos_hbm, sin_hbm, o_ref,
    w_ref, gain_ref, qg_ref, kg_ref, cos_ref, sin_ref, landing, wa, wb, wc, h_ref, q_ref, xn, acc, kvs, kvb, qn, qb, ob,
    in_s, a_s, a_r, row_s, row_r, p_s, p_r, az_s, az_r, z_s, z_r, l_s, l_r, x_s, x_r,
    q_s, q_r, kv_s, kv_r, halo_s, o_s, o_r,
):
    c = lax.axis_index("dp")
    t = lax.axis_index("ctx")
    z = lax.div(t, PLANE)
    i = lax.rem(t, PLANE)
    y = lax.div(i, NX)
    x = lax.rem(i, NX)
    yh = lax.div(y, 2)
    yl = lax.rem(y, 2)
    block_len = cos_ref.shape[0]

    def chip(zz, yy, xx):
        return zz * PLANE + yy * NX + xx

    def step(v, d, n):
        return lax.rem(v + (d % n), n)

    sibling = (1 - c, t)
    pending = []

    def remote(src, dst, send, recv, device):
        return pltpu.make_async_remote_copy(
            src_ref=src, dst_ref=dst, send_sem=send, recv_sem=recv,
            device_id=device, device_id_type=MESH,
        )

    def push(src, dst, send, recv, device):
        copy = remote(src, dst, send, recv, device)
        copy.start()
        pending.append(copy)

    def arrived(region, recv):
        pltpu.make_async_copy(region, region, recv).wait()

    loads = [
        pltpu.make_async_copy(src, dst, in_s.at[n])
        for n, (src, dst) in enumerate((
            (w_hbm, w_ref), (q_hbm, q_ref), (qg_hbm, qg_ref.at[0]), (kg_hbm, kg_ref.at[0]),
            (cos_hbm, cos_ref), (sin_hbm, sin_ref), (h_hbm, h_ref), (gain_hbm, gain_ref.at[0]),
        ))
    ]
    for load in loads:
        load.start()

    barrier = pltpu.get_barrier_semaphore()
    for r in range(1, 2 * PLANE):
        dev = (lax.rem(c + r % 2, 2), z * PLANE + lax.rem(i + r // 2, PLANE))
        pl.semaphore_signal(barrier, inc=1, device_id=dev, device_id_type=MESH)
    for d in (1, -1):
        pl.semaphore_signal(
            barrier, inc=1, device_id=(c, chip(step(z, d, NZ), y, x)), device_id_type=MESH
        )


    def query_heads(s):
        for h in range(16):
            head = q_ref[s, :, h * HD:(h + 1) * HD].astype(F32)
            qn[s, :, h * HD:(h + 1) * HD] = (head_rotary(head, qg, cos, sin) * SCALE).astype(BF)

    loads[0].wait()
    pl.semaphore_wait(barrier, 2 * PLANE - 1 + 2)

    j = yl * NX + x
    for r in range(1, MEMBERS):
        peer = lax.rem(j + r, MEMBERS)
        pyl, px = lax.div(peer, NX), lax.rem(peer, NX)
        col = pl.multiple_of(pyl * 1024 + c * 512 + px * HD, HD)
        push(
            w_ref.at[:, pl.ds(col, HD)], landing.at[j], a_s.at[r], a_r.at[r],
            (c, chip(z, yh * 2 + pyl, px)),
        )
    col = pl.multiple_of(yl * 1024 + c * 512 + x * HD, HD)
    landing[j] = w_ref[:, pl.ds(col, HD)]

    def q_pieces(start):
        for k in range(8):
            for kk in range(2):
                low = lax.rem(i + k, 8)
                core = lax.rem(c + kk, 2)
                s = lax.div(low, 4)
                h = core * 4 + lax.rem(low, 4)
                src = qn.at[s, :, pl.ds(pl.multiple_of(h * 256, 256), 256)]
                dst = qb.at[i]
                dev = (core, z * PLANE + c * 8 + low)
                send, recv = q_s.at[k * 2 + kk], q_r.at[i]
                if k == 0 and kk == 0:
                    here = lax.div(i, 8) == c

                    @pl.when(here)
                    def _():
                        if start:
                            pltpu.make_async_copy(src, dst, recv).start()

                    @pl.when(jnp.logical_not(here))
                    def _():
                        copy = remote(src, dst, send, recv, dev)
                        copy.start() if start else copy.wait_send()
                else:
                    copy = remote(src, dst, send, recv, dev)
                    copy.start() if start else copy.wait_send()

    for load in loads[1:6]:
        load.wait()
    cos, sin, qg, kg = cos_ref[...], sin_ref[...], qg_ref[...], kg_ref[...]
    query_heads(0)
    for r in range(1, MEMBERS):
        arrived(landing.at[lax.rem(j + MEMBERS - r, MEMBERS)], a_r.at[r])
    rows = jnp.concatenate([landing[m].astype(F32) for m in range(MEMBERS)], axis=0).astype(BF)
    wa[z, x, y] = rows[:ROWS_A]
    wb[y, z, x] = rows[ROWS_A:ROWS_A + ROWS_B]
    wc[x, z, y] = rows[ROWS_A + ROWS_B:]

    for d in (1, 3, 2):
        push(wb.at[y, z, x], wb.at[y, z, x], row_s.at[d], row_r.at[d], (c, chip(z, y, step(x, d, NX))))
        push(wc.at[x, z, y], wc.at[x, z, y], row_s.at[4 + d], row_r.at[4 + d], (c, chip(z, step(y, d, NY), x)))
    for d in (1, 3, 2):
        push(wa.at[z, x, y], wa.at[z, x, y], row_s.at[8 + d], row_r.at[8 + d], (c, chip(z, step(y, d, NY), x)))
    query_heads(1)
    for d in (1, 3, 2):
        arrived(wb.at[y, z, step(x, -d, NX)], row_r.at[d])
        arrived(wc.at[x, z, step(y, -d, NY)], row_r.at[4 + d])

    def chunk(part, line, zz):
        return wb.at[line, zz] if part == 0 else wc.at[line, zz]

    def half(part, line, zz, which):
        ref = wb if part == 0 else wc
        return ref.at[line, zz, pl.ds(2 * which, 2)]

    def line_device(part, d):
        if part == 0:
            return (c, chip(z, step(y, d, NY), x))
        return (c, chip(z, y, step(x, d, NX)))

    own = (y, x)
    along = (NY, NX)

    def z_sem(part, way, d):
        return (part * 2 + way) * 5 + d

    def l_sem(part, way, kind, slot):
        return ((part * 2 + way) * 2 + kind) * 8 + slot

    def z_send(part, zz, way, d):
        dev = (c, chip(step(z, 1 if way == 0 else -1, NZ), y, x))
        ref = chunk(part, own[part], zz) if d < 4 else half(part, own[part], zz, way)
        n = z_sem(part, way, d)
        push(ref, ref, z_s.at[n], z_r.at[n], dev)

    def z_wait(part, zz, way, d):
        ref = chunk(part, own[part], zz) if d < 4 else half(part, own[part], zz, way)
        arrived(ref, z_r.at[z_sem(part, way, d)])

    def line_send(part, zz, slot):
        for way, d in ((0, 1), (1, -1)):
            ref = chunk(part, own[part], zz)
            n = l_sem(part, way, 0, slot)
            push(ref, ref, l_s.at[n], l_r.at[n], line_device(part, d))

    def line_relay(part, zz, slot):
        for way, d in ((0, 1), (1, -1)):
            line = step(own[part], -d, along[part])
            arrived(chunk(part, line, zz), l_r.at[l_sem(part, way, 0, slot)])
            ref = half(part, line, zz, way)
            n = l_sem(part, way, 1, slot)
            push(ref, ref, l_s.at[n], l_r.at[n], line_device(part, d))

    def line_finish(part, zz, slot):
        for way in range(2):
            line = step(own[part], 2, along[part])
            arrived(half(part, line, zz, way), l_r.at[l_sem(part, way, 1, slot)])

    def slots(k):
        if k == 0:
            return [(z, 0)]
        if k == 4:
            return [(step(z, 4, NZ), 7)]
        return [(step(z, -k, NZ), k), (step(z, k, NZ), 3 + k)]

    def norm_rows():
        def one(n, carry):
            at = pl.multiple_of(n * 16, 16)
            s, row = lax.div(at, block_len), pl.multiple_of(lax.rem(at, block_len), 16)
            v = h_ref[s, pl.ds(row, 16), :].astype(F32)
            mean = jnp.mean(v * v, axis=-1, keepdims=True)
            v = v * lax.rsqrt(mean + EPS) * gain_ref[...]
            pad = jnp.zeros((16, PLANE_LANES - PLANE_ROWS), F32)
            for zz in range(NZ):
                piece = jnp.concatenate([v[:, zz * PLANE_ROWS:(zz + 1) * PLANE_ROWS], pad], axis=1)
                xn[zz, c, pl.ds(at, 16), :] = piece.astype(BF)
            return carry

        lax.fori_loop(0, 2 * block_len // 16, one, 0)

    def plane_across():
        for d in (1, 3, 2):
            arrived(wa.at[z, x, step(y, -d, NY)], row_r.at[8 + d])
        for d in (1, 3, 2):
            push(wa.at[z, x], wa.at[z, x], p_s.at[d], p_r.at[d], (c, chip(z, y, step(x, d, NX))))

    def plane_send(zz, way, d):
        dev = (c, chip(step(z, 1 if way == 0 else -1, NZ), y, x))
        for which in range(2):
            if d < 4 or which == way:
                ref = wa.at[zz, pl.ds(2 * which, 2)]
                n = (way * 2 + which) * 5 + d
                push(ref, ref, az_s.at[n], az_r.at[n], dev)

    def plane_relay(k):
        if k == 0:
            for d in (1, 3, 2):
                arrived(wa.at[z, step(x, -d, NX)], p_r.at[d])
            plane_send(z, 0, 1)
            plane_send(z, 1, 1)
            return
        dev = [(c, chip(step(z, 1 if way == 0 else -1, NZ), y, x)) for way in range(2)]
        for which in range(2):
            for way in range(2):
                zz = step(z, -k if way == 0 else k, NZ)
                if k == 4 and which != way:
                    continue
                ref = wa.at[zz, pl.ds(2 * which, 2)]
                n = (way * 2 + which) * 5 + k
                arrived(ref, az_r.at[n])
                if k < 3 or (k == 3 and which == way):
                    push(ref, ref, az_s.at[n + 1], az_r.at[n + 1], dev[way])

    def project(zz, first):
        def pair(n, carry):
            nyl, nx = lax.div(n, 2), 2 * lax.rem(n, 2)
            pieces = []
            for hi in range(2):
                ny = 2 * hi + nyl
                pieces.append(jnp.concatenate([wa[zz, nx, ny], wa[zz, nx + 1, ny]], axis=1))
                pieces.append(jnp.concatenate([wb[ny, zz, nx], wb[ny, zz, nx + 1]], axis=1))
                pieces.append(jnp.concatenate([wc[nx, zz, ny], wc[nx + 1, zz, ny]], axis=1))
            right = jnp.concatenate(pieces, axis=0)
            for g in range(2):
                term = jnp.dot(xn[zz, g, :, :PLANE_ROWS], right, preferred_element_type=F32)
                acc[n, g] = term if first else acc[n, g] + term
            return carry

        lax.fori_loop(0, 4, pair, 0)

    def complete(k):
        for zz, slot in slots(k):
            for part in range(2):
                line_finish(part, zz, slot)
            project(zz, k == 0)

    for k in range(5):
        if k > 0:
            for way, (zz, _) in enumerate(slots(k) if k < 4 else slots(k) * 2):
                for part in range(2):
                    z_wait(part, zz, way, k)
                    if k < 4:
                        z_send(part, zz, way, k + 1)
        else:
            for way in range(2):
                for part in range(2):
                    z_send(part, z, way, 1)
        for zz, slot in slots(k):
            for part in range(2):
                line_send(part, zz, slot)
        if k == 1:
            plane_relay(0)
        if k == 0:
            plane_across()
            q_pieces(True)
            for load in loads[6:]:
                load.wait()
            norm_rows()
            push(xn.at[:, c], xn.at[:, c], x_s, x_r, sibling)
        if k > 0:
            for zz, slot in slots(k - 1):
                for part in range(2):
                    line_relay(part, zz, slot)
            if k > 1:
                plane_relay(k - 1)
        if k == 3:
            arrived(xn.at[:, 1 - c], x_r)
        if k > 2:
            complete(k - 3)
    for zz, slot in slots(4):
        for part in range(2):
            line_relay(part, zz, slot)
    complete(2)
    complete(3)
    plane_relay(4)
    complete(4)

    def kv_pieces(e, start):
        for k in range(8):
            q = lax.rem(i + k, 8)
            u = lax.div(q, 4) * 8 + lax.rem(lax.div(q, 2), 2) * 4 + 2 * e + lax.rem(q, 2)
            src, dst = kvs.at[u], kvb.at[SLABS + i]
            send, recv = kv_s.at[e * 8 + k], kv_r.at[SLABS + i]
            here = u == i

            @pl.when(here)
            def _():
                if start:
                    pltpu.make_async_copy(src, dst, recv).start()

            @pl.when(jnp.logical_not(here))
            def _():
                copy = remote(src, dst, send, recv, (c, z * PLANE + u))
                copy.start() if start else copy.wait_send()

    for e in range(2):
        for g in range(2):
            for s in range(2):
                for b in range(2):
                    head = acc[e, g, s * block_len:(s + 1) * block_len, b * HD:(b + 1) * HD]
                    kvs[g * 8 + s * 4 + 2 * e + b, :, :HD] = head_rotary(head, kg, cos, sin).astype(BF)
        for g in range(2):
            for s in range(2):
                for b in range(2):
                    head = acc[2 + e, g, s * block_len:(s + 1) * block_len, b * HD:(b + 1) * HD]
                    kvs[g * 8 + s * 4 + 2 * e + b, :, HD:] = head.astype(BF)
        kv_pieces(e, True)

    for n in range(SLABS):
        arrived(kvb.at[16 + n], kv_r.at[16 + n])

        @pl.when(z < NZ - 1)
        def _(n=n):
            remote(
                kvb.at[16 + n], kvb.at[n], halo_s.at[n], kv_r.at[n], (c, t + PLANE)
            ).start()
    for n in range(SLABS):
        arrived(kvb.at[8 + n], kv_r.at[8 + n])
    for n in range(PLANE):
        arrived(qb.at[n], q_r.at[n])

    unit_g = lax.div(i, 8)
    unit_s = lax.rem(lax.div(i, 4), 2)
    unit_h = c * 4 + lax.rem(i, 4)
    out_col = pl.multiple_of(unit_h * 256, 256)
    row_at = lax.broadcasted_iota(jnp.int32, (2 * HD, HD), 0)
    row_at = jnp.where(row_at >= HD, row_at - HD, row_at)
    col_at = lax.broadcasted_iota(jnp.int32, (2 * HD, HD), 1)

    def out_copy(slab):
        return remote(
            ob.at[slab], o_ref.at[unit_s, :, pl.ds(out_col, 256)],
            o_s.at[slab], o_r.at[unit_s * 8 + unit_h], (unit_g, z * PLANE + slab),
        )

    def attend(slab, first_half):
        q = jnp.concatenate([qb[slab, :, :HD], qb[slab, :, HD:]], axis=0)
        total = jnp.zeros((2 * HD, 1), F32)
        out = jnp.zeros((2 * HD, HD), F32)
        for b in range(9):
            keys = kvb[slab + b, :, :HD]
            values = kvb[slab + b, :, HD:]
            scores = lax.dot_general(q, keys, (((1,), (1,)), ((), ())), preferred_element_type=F32)
            weight = jnp.exp(scores)
            if b == 0:
                weight = jnp.where(col_at > row_at, weight, 0.0)
            if b == 8:
                weight = jnp.where(col_at <= row_at, weight, 0.0)
            elif first_half:
                seen = jnp.logical_or(z > 0, slab + b >= SLABS)
                weight = jnp.where(seen, weight, 0.0)
            total = total + jnp.sum(weight, axis=-1, keepdims=True)
            out = out + jnp.dot(weight.astype(BF), values, preferred_element_type=F32)
        out = (out / total).astype(BF)
        ob[slab] = jnp.concatenate([out[:HD], out[HD:]], axis=1)
        here = jnp.logical_and(unit_g == c, slab == i)

        @pl.when(here)
        def _():
            pltpu.make_async_copy(
                ob.at[slab], o_ref.at[unit_s, :, pl.ds(out_col, 256)], o_r.at[unit_s * 8 + unit_h]
            ).start()

        @pl.when(jnp.logical_not(here))
        def _():
            out_copy(slab).start()

    def late(n, carry):
        attend(8 + lax.rem(i + n, 8), False)
        return carry

    lax.fori_loop(0, 8, late, 0)

    for n in range(SLABS):
        @pl.when(z > 0)
        def _(n=n):
            arrived(kvb.at[n], kv_r.at[n])

        @pl.when(z == 0)
        def _(n=n):
            kvb[n] = jnp.zeros((HD, 2 * HD), BF)

    def early(n, carry):
        attend(lax.rem(i + n, 8), True)
        return carry

    lax.fori_loop(0, 8, early, 0)

    for s in range(2):
        for h in range(8):
            arrived(o_ref.at[s, :, pl.ds(h * 256, 256)], o_r.at[s * 8 + h])

    for copy in pending:
        copy.wait_send()
    q_pieces(False)
    kv_pieces(0, False)
    kv_pieces(1, False)
    for n in range(SLABS):
        @pl.when(z < NZ - 1)
        def _(n=n):
            remote(
                kvb.at[16 + n], kvb.at[n], halo_s.at[n], kv_r.at[n], (c, t + PLANE)
            ).wait_send()
    for slab in range(PLANE):
        @pl.when(jnp.logical_not(jnp.logical_and(unit_g == c, slab == i)))
        def _(slab=slab):
            out_copy(slab).wait_send()


def body(hidden, queries, input_gain, kv_weight, query_gain, key_gain):
    block_len = hidden.shape[1]
    model_width = hidden.shape[2]
    positions = lax.axis_index("ctx") * block_len + jnp.arange(block_len, dtype=jnp.int32)
    exponent = 2.0 * jnp.arange(HD // 2, dtype=F32) / HD
    inverse = jnp.power(10000.0, -exponent)
    angles = positions.astype(F32)[:, None] * inverse[None, :]
    cos, sin = jnp.cos(angles), jnp.sin(angles)
    cos = jnp.concatenate([cos, cos], axis=1)
    sin = jnp.concatenate([-sin, sin], axis=1)
    dma = pltpu.SemaphoreType.DMA
    return pl.pallas_call(
        kernel,
        out_shape=pltpu.VMEM(queries.shape, BF),
        in_specs=[
            pl.BlockSpec(memory_space=pl.ANY) for n in range(8)
        ],
        out_specs=pl.BlockSpec(memory_space=pltpu.VMEM),
        scratch_shapes=[
            pltpu.VMEM(kv_weight.shape, BF),
            pltpu.VMEM((1, model_width), F32),
            pltpu.VMEM((1, HD), F32),
            pltpu.VMEM((1, HD), F32),
            pltpu.VMEM((block_len, HD), F32),
            pltpu.VMEM((block_len, HD), F32),
            pltpu.VMEM((MEMBERS, 42, HD), BF),
            pltpu.VMEM((NZ, NX, NY, ROWS_A, HD), BF),
            pltpu.VMEM((NY, NZ, NX, ROWS_B, HD), BF),
            pltpu.VMEM((NX, NZ, NY, ROWS_C, HD), BF),
            pltpu.VMEM(hidden.shape, BF),
            pltpu.VMEM(queries.shape, BF),
            pltpu.VMEM((NZ, 2, 2 * block_len, PLANE_LANES), BF),
            pltpu.VMEM((4, 2, 2 * block_len, 256), F32),
            pltpu.VMEM((16, HD, 256), BF),
            pltpu.VMEM((24, HD, 256), BF),
            pltpu.VMEM(queries.shape, BF),
            pltpu.VMEM((16, HD, 256), BF),
            pltpu.VMEM((16, HD, 256), BF),
            dma((8,)), dma((8,)), dma((8,)), dma((12,)), dma((12,)), dma((4,)), dma((4,)),
            dma((20,)), dma((20,)), dma((20,)), dma((20,)),
            dma((64,)), dma((64,)), dma, dma,
            dma((16,)), dma((16,)), dma((16,)), dma((24,)), dma((8,)), dma((16,)), dma((16,)),
        ],
        compiler_params=pltpu.CompilerParams(
            collective_id=0, has_side_effects=True, vmem_limit_bytes=60 << 20
        ),
    )(
        kv_weight, hidden, queries, input_gain, query_gain, key_gain, cos, sin,
    )


def solution(mesh):
    return jax.shard_map(
        body,
        mesh=mesh,
        in_specs=(P("dp", "ctx", None), P("dp", "ctx", None), P(), P("ctx", None), P(), P()),
        out_specs=P("dp", "ctx", None),
        check_vma=False,
    )
```

```python
import jax
import jax.numpy as jnp
from jax import lax
from jax.experimental import pallas as pl
from jax.experimental.pallas import tpu as pltpu
from jax.sharding import PartitionSpec as P

HD = 128
WINDOW = 1024
EPS = 1e-6
SCALE = 168.0 ** -0.5
NX, NY, NZ = 4, 4, 8
PLANE = NX * NY
SLABS = WINDOW // HD
MEMBERS = 8
ROWS_A, ROWS_B, ROWS_C = 80, 128, 128
PLANE_ROWS = 2 * (ROWS_A + ROWS_B + ROWS_C)
PLANE_LANES = 768
BF = jnp.bfloat16
F32 = jnp.float32
MESH = pl.DeviceIdType.MESH


def head_rotary(head, gain, cos, sin):
    mean = jnp.mean(head * head, axis=-1, keepdims=True)
    unit = head * lax.rsqrt(mean + EPS) * gain
    return unit * cos + pltpu.roll(unit, 64, 1) * sin


def kernel(
    w_hbm, h_hbm, q_hbm, gain_hbm, qg_hbm, kg_hbm, cos_hbm, sin_hbm, o_ref,
    w_ref, gain_ref, qg_ref, kg_ref, cos_ref, sin_ref, landing, wa, wb, wc, h_ref, q_ref, xn, acc, kvs, kvb, qn, qb, ob,
    in_s, a_s, a_r, row_s, row_r, p_s, p_r, az_s, az_r, z_s, z_r, l_s, l_r, x_s, x_r,
    q_s, q_r, kv_s, kv_r, halo_s, o_s, o_r,
):
    c = lax.axis_index("dp")
    t = lax.axis_index("ctx")
    z = lax.div(t, PLANE)
    i = lax.rem(t, PLANE)
    y = lax.div(i, NX)
    x = lax.rem(i, NX)
    yh = lax.div(y, 2)
    yl = lax.rem(y, 2)
    block_len = cos_ref.shape[0]

    def chip(zz, yy, xx):
        return zz * PLANE + yy * NX + xx

    def step(v, d, n):
        return lax.rem(v + (d % n), n)

    sibling = (1 - c, t)
    pending = []

    def remote(src, dst, send, recv, device):
        return pltpu.make_async_remote_copy(
            src_ref=src, dst_ref=dst, send_sem=send, recv_sem=recv,
            device_id=device, device_id_type=MESH,
        )

    def push(src, dst, send, recv, device):
        copy = remote(src, dst, send, recv, device)
        copy.start()
        pending.append(copy)

    def arrived(region, recv):
        pltpu.make_async_copy(region, region, recv).wait()

    loads = [
        pltpu.make_async_copy(src, dst, in_s.at[n])
        for n, (src, dst) in enumerate((
            (w_hbm, w_ref), (q_hbm, q_ref), (qg_hbm, qg_ref.at[0]), (kg_hbm, kg_ref.at[0]),
            (cos_hbm, cos_ref), (sin_hbm, sin_ref), (h_hbm, h_ref), (gain_hbm, gain_ref.at[0]),
        ))
    ]
    for load in loads:
        load.start()

    barrier = pltpu.get_barrier_semaphore()
    for r in range(1, 2 * PLANE):
        dev = (lax.rem(c + r % 2, 2), z * PLANE + lax.rem(i + r // 2, PLANE))
        pl.semaphore_signal(barrier, inc=1, device_id=dev, device_id_type=MESH)
    for d in (1, -1):
        pl.semaphore_signal(
            barrier, inc=1, device_id=(c, chip(step(z, d, NZ), y, x)), device_id_type=MESH
        )


    def query_heads(s):
        for h in range(16):
            head = q_ref[s, :, h * HD:(h + 1) * HD].astype(F32)
            qn[s, :, h * HD:(h + 1) * HD] = (head_rotary(head, qg, cos, sin) * SCALE).astype(BF)

    loads[0].wait()
    pl.semaphore_wait(barrier, 2 * PLANE - 1 + 2)

    j = yl * NX + x
    for r in range(1, MEMBERS):
        peer = lax.rem(j + r, MEMBERS)
        pyl, px = lax.div(peer, NX), lax.rem(peer, NX)
        col = pl.multiple_of(pyl * 1024 + c * 512 + px * HD, HD)
        push(
            w_ref.at[:, pl.ds(col, HD)], landing.at[j], a_s.at[r], a_r.at[r],
            (c, chip(z, yh * 2 + pyl, px)),
        )
    col = pl.multiple_of(yl * 1024 + c * 512 + x * HD, HD)
    landing[j] = w_ref[:, pl.ds(col, HD)]

    def q_pieces(start):
        for k in range(8):
            for kk in range(2):
                low = lax.rem(i + k, 8)
                core = lax.rem(c + kk, 2)
                s = lax.div(low, 4)
                h = core * 4 + lax.rem(low, 4)
                src = qn.at[s, :, pl.ds(pl.multiple_of(h * 256, 256), 256)]
                dst = qb.at[i]
                dev = (core, z * PLANE + c * 8 + low)
                send, recv = q_s.at[k * 2 + kk], q_r.at[i]
                if k == 0 and kk == 0:
                    here = lax.div(i, 8) == c

                    @pl.when(here)
                    def _():
                        if start:
                            pltpu.make_async_copy(src, dst, recv).start()

                    @pl.when(jnp.logical_not(here))
                    def _():
                        copy = remote(src, dst, send, recv, dev)
                        copy.start() if start else copy.wait_send()
                else:
                    copy = remote(src, dst, send, recv, dev)
                    copy.start() if start else copy.wait_send()

    for load in loads[1:6]:
        load.wait()
    cos, sin, qg, kg = cos_ref[...], sin_ref[...], qg_ref[...], kg_ref[...]
    query_heads(0)
    for r in range(1, MEMBERS):
        arrived(landing.at[lax.rem(j + MEMBERS - r, MEMBERS)], a_r.at[r])
    rows = jnp.concatenate([landing[m].astype(F32) for m in range(MEMBERS)], axis=0).astype(BF)
    wa[z, x, y] = rows[:ROWS_A]
    wb[y, z, x] = rows[ROWS_A:ROWS_A + ROWS_B]
    wc[x, z, y] = rows[ROWS_A + ROWS_B:]

    for d in (1, 3, 2):
        push(wb.at[y, z, x], wb.at[y, z, x], row_s.at[d], row_r.at[d], (c, chip(z, y, step(x, d, NX))))
        push(wc.at[x, z, y], wc.at[x, z, y], row_s.at[4 + d], row_r.at[4 + d], (c, chip(z, step(y, d, NY), x)))
    for d in (1, 3, 2):
        push(wa.at[z, x, y], wa.at[z, x, y], row_s.at[8 + d], row_r.at[8 + d], (c, chip(z, step(y, d, NY), x)))
    query_heads(1)
    for d in (1, 3, 2):
        arrived(wb.at[y, z, step(x, -d, NX)], row_r.at[d])
        arrived(wc.at[x, z, step(y, -d, NY)], row_r.at[4 + d])

    def chunk(part, line, zz):
        return wb.at[line, zz] if part == 0 else wc.at[line, zz]

    def half(part, line, zz, which):
        ref = wb if part == 0 else wc
        return ref.at[line, zz, pl.ds(2 * which, 2)]

    def line_device(part, d):
        if part == 0:
            return (c, chip(z, step(y, d, NY), x))
        return (c, chip(z, y, step(x, d, NX)))

    own = (y, x)
    along = (NY, NX)

    def z_sem(part, way, d):
        return (part * 2 + way) * 5 + d

    def l_sem(part, way, kind, slot):
        return ((part * 2 + way) * 2 + kind) * 8 + slot

    def z_send(part, zz, way, d):
        dev = (c, chip(step(z, 1 if way == 0 else -1, NZ), y, x))
        ref = chunk(part, own[part], zz) if d < 4 else half(part, own[part], zz, way)
        n = z_sem(part, way, d)
        push(ref, ref, z_s.at[n], z_r.at[n], dev)

    def z_wait(part, zz, way, d):
        ref = chunk(part, own[part], zz) if d < 4 else half(part, own[part], zz, way)
        arrived(ref, z_r.at[z_sem(part, way, d)])

    def line_send(part, zz, slot):
        for way, d in ((0, 1), (1, -1)):
            ref = chunk(part, own[part], zz)
            n = l_sem(part, way, 0, slot)
            push(ref, ref, l_s.at[n], l_r.at[n], line_device(part, d))

    def line_relay(part, zz, slot):
        for way, d in ((0, 1), (1, -1)):
            line = step(own[part], -d, along[part])
            arrived(chunk(part, line, zz), l_r.at[l_sem(part, way, 0, slot)])
            ref = half(part, line, zz, way)
            n = l_sem(part, way, 1, slot)
            push(ref, ref, l_s.at[n], l_r.at[n], line_device(part, d))

    def line_finish(part, zz, slot):
        for way in range(2):
            line = step(own[part], 2, along[part])
            arrived(half(part, line, zz, way), l_r.at[l_sem(part, way, 1, slot)])

    def slots(k):
        if k == 0:
            return [(z, 0)]
        if k == 4:
            return [(step(z, 4, NZ), 7)]
        return [(step(z, -k, NZ), k), (step(z, k, NZ), 3 + k)]

    def norm_rows():
        def one(n, carry):
            at = pl.multiple_of(n * 16, 16)
            s, row = lax.div(at, block_len), pl.multiple_of(lax.rem(at, block_len), 16)
            v = h_ref[s, pl.ds(row, 16), :].astype(F32)
            mean = jnp.mean(v * v, axis=-1, keepdims=True)
            v = v * lax.rsqrt(mean + EPS) * gain_ref[...]
            pad = jnp.zeros((16, PLANE_LANES - PLANE_ROWS), F32)
            for zz in range(NZ):
                piece = jnp.concatenate([v[:, zz * PLANE_ROWS:(zz + 1) * PLANE_ROWS], pad], axis=1)
                xn[zz, c, pl.ds(at, 16), :] = piece.astype(BF)
            return carry

        lax.fori_loop(0, 2 * block_len // 16, one, 0)

    def plane_across():
        for d in (1, 3, 2):
            arrived(wa.at[z, x, step(y, -d, NY)], row_r.at[8 + d])
        for d in (1, 3, 2):
            push(wa.at[z, x], wa.at[z, x], p_s.at[d], p_r.at[d], (c, chip(z, y, step(x, d, NX))))

    def plane_send(zz, way, d):
        dev = (c, chip(step(z, 1 if way == 0 else -1, NZ), y, x))
        for which in range(2):
            if d < 4 or which == way:
                ref = wa.at[zz, pl.ds(2 * which, 2)]
                n = (way * 2 + which) * 5 + d
                push(ref, ref, az_s.at[n], az_r.at[n], dev)

    def plane_relay(k):
        if k == 0:
            for d in (1, 3, 2):
                arrived(wa.at[z, step(x, -d, NX)], p_r.at[d])
            plane_send(z, 0, 1)
            plane_send(z, 1, 1)
            return
        dev = [(c, chip(step(z, 1 if way == 0 else -1, NZ), y, x)) for way in range(2)]
        for which in range(2):
            for way in range(2):
                zz = step(z, -k if way == 0 else k, NZ)
                if k == 4 and which != way:
                    continue
                ref = wa.at[zz, pl.ds(2 * which, 2)]
                n = (way * 2 + which) * 5 + k
                arrived(ref, az_r.at[n])
                if k < 3 or (k == 3 and which == way):
                    push(ref, ref, az_s.at[n + 1], az_r.at[n + 1], dev[way])

    def rows_of(zz, nyl, nx):
        pieces = []
        for hi in range(2):
            ny = 2 * hi + nyl
            pieces.append(jnp.concatenate([wa[zz, nx, ny], wa[zz, nx + 1, ny]], axis=1))
            pieces.append(jnp.concatenate([wb[ny, zz, nx], wb[ny, zz, nx + 1]], axis=1))
            pieces.append(jnp.concatenate([wc[nx, zz, ny], wc[nx + 1, zz, ny]], axis=1))
        return jnp.concatenate(pieces, axis=0)

    def project(planes, first):
        def pair(n, carry):
            nyl, nx = lax.div(n, 2), 2 * lax.rem(n, 2)
            for g in range(2):
                term = None if first else acc[n, g]
                for zz in planes:
                    more = jnp.dot(
                        xn[zz, g, :, :PLANE_ROWS], rows_of(zz, nyl, nx), preferred_element_type=F32
                    )
                    term = more if term is None else term + more
                acc[n, g] = term
            return carry

        lax.fori_loop(0, 4, pair, 0)

    def complete(k):
        for zz, slot in slots(k):
            for part in range(2):
                line_finish(part, zz, slot)
        project([zz for zz, _ in slots(k)], k == 0)

    for k in range(5):
        if k > 0:
            for way, (zz, _) in enumerate(slots(k) if k < 4 else slots(k) * 2):
                for part in range(2):
                    z_wait(part, zz, way, k)
                    if k < 4:
                        z_send(part, zz, way, k + 1)
        else:
            for way in range(2):
                for part in range(2):
                    z_send(part, z, way, 1)
        for zz, slot in slots(k):
            for part in range(2):
                line_send(part, zz, slot)
        if k == 1:
            plane_relay(0)
        if k == 0:
            plane_across()
            q_pieces(True)
            for load in loads[6:]:
                load.wait()
            norm_rows()
            push(xn.at[:, c], xn.at[:, c], x_s, x_r, sibling)
        if k > 0:
            for zz, slot in slots(k - 1):
                for part in range(2):
                    line_relay(part, zz, slot)
            if k > 1:
                plane_relay(k - 1)
        if k == 3:
            arrived(xn.at[:, 1 - c], x_r)
        if k > 2:
            complete(k - 3)
    for zz, slot in slots(4):
        for part in range(2):
            line_relay(part, zz, slot)
    complete(2)
    complete(3)
    plane_relay(4)
    complete(4)

    def kv_pieces(start):
        for k in range(PLANE):
            u = lax.rem(i + k, PLANE)
            src, dst = kvs.at[u], kvb.at[SLABS + i]
            send, recv = kv_s.at[k], kv_r.at[SLABS + i]
            if k > 0:
                copy = remote(src, dst, send, recv, (c, z * PLANE + u))
                copy.start() if start else copy.wait_send()
            elif start:
                pltpu.make_async_copy(src, dst, recv).start()

    for g in range(2):
        for s in range(2):
            for h in range(4):
                rows, lanes = slice(s * block_len, (s + 1) * block_len), slice(h % 2 * HD, (h % 2 + 1) * HD)
                u = g * 8 + s * 4 + h
                kvs[u, :, :HD] = head_rotary(acc[h // 2, g, rows, lanes], kg, cos, sin).astype(BF)
                kvs[u, :, HD:] = acc[2 + h // 2, g, rows, lanes].astype(BF)
    kv_pieces(True)

    def halo(src):
        n = src - SLABS
        return remote(kvb.at[16 + n], kvb.at[n], halo_s.at[n], kv_r.at[n], (c, t + PLANE))

    def receive(k, carry):
        src = lax.rem(i + PLANE - k, PLANE)
        arrived(kvb.at[SLABS + src], kv_r.at[SLABS + src])

        @pl.when(jnp.logical_and(src >= SLABS, z < NZ - 1))
        def _():
            halo(src).start()

        return carry

    lax.fori_loop(0, PLANE, receive, 0)
    for n in range(PLANE):
        arrived(qb.at[n], q_r.at[n])

    unit_g = lax.div(i, 8)
    unit_s = lax.rem(lax.div(i, 4), 2)
    unit_h = c * 4 + lax.rem(i, 4)
    out_col = pl.multiple_of(unit_h * 256, 256)
    row_at = lax.broadcasted_iota(jnp.int32, (2 * HD, HD), 0)
    row_at = jnp.where(row_at >= HD, row_at - HD, row_at)
    col_at = lax.broadcasted_iota(jnp.int32, (2 * HD, HD), 1)

    def out_copy(slab):
        return remote(
            ob.at[slab], o_ref.at[unit_s, :, pl.ds(out_col, 256)],
            o_s.at[slab], o_r.at[unit_s * 8 + unit_h], (unit_g, z * PLANE + slab),
        )

    def attend(slab, first_half):
        q = jnp.concatenate([qb[slab, :, :HD], qb[slab, :, HD:]], axis=0)
        total = jnp.zeros((2 * HD, 1), F32)
        out = jnp.zeros((2 * HD, HD), F32)
        for b in range(9):
            keys = kvb[slab + b, :, :HD]
            values = kvb[slab + b, :, HD:]
            scores = lax.dot_general(q, keys, (((1,), (1,)), ((), ())), preferred_element_type=F32)
            weight = jnp.exp(scores)
            if b == 0:
                weight = jnp.where(col_at > row_at, weight, 0.0)
            if b == 8:
                weight = jnp.where(col_at <= row_at, weight, 0.0)
            elif first_half:
                seen = jnp.logical_or(z > 0, slab + b >= SLABS)
                weight = jnp.where(seen, weight, 0.0)
            total = total + jnp.sum(weight, axis=-1, keepdims=True)
            out = out + jnp.dot(weight.astype(BF), values, preferred_element_type=F32)
        out = (out / total).astype(BF)
        ob[slab] = jnp.concatenate([out[:HD], out[HD:]], axis=1)
        here = jnp.logical_and(unit_g == c, slab == i)

        @pl.when(here)
        def _():
            pltpu.make_async_copy(
                ob.at[slab], o_ref.at[unit_s, :, pl.ds(out_col, 256)], o_r.at[unit_s * 8 + unit_h]
            ).start()

        @pl.when(jnp.logical_not(here))
        def _():
            out_copy(slab).start()

    def late(n, carry):
        attend(8 + lax.rem(i + n, 8), False)
        return carry

    lax.fori_loop(0, 8, late, 0)

    for n in range(SLABS):
        @pl.when(z > 0)
        def _(n=n):
            arrived(kvb.at[n], kv_r.at[n])

        @pl.when(z == 0)
        def _(n=n):
            kvb[n] = jnp.zeros((HD, 2 * HD), BF)

    def early(n, carry):
        attend(lax.rem(i + n, 8), True)
        return carry

    lax.fori_loop(0, 8, early, 0)

    for s in range(2):
        for h in range(8):
            arrived(o_ref.at[s, :, pl.ds(h * 256, 256)], o_r.at[s * 8 + h])

    for copy in pending:
        copy.wait_send()
    q_pieces(False)
    kv_pieces(False)
    for n in range(SLABS):
        @pl.when(z < NZ - 1)
        def _(n=n):
            halo(SLABS + n).wait_send()
    for slab in range(PLANE):
        @pl.when(jnp.logical_not(jnp.logical_and(unit_g == c, slab == i)))
        def _(slab=slab):
            out_copy(slab).wait_send()


def body(hidden, queries, input_gain, kv_weight, query_gain, key_gain):
    block_len = hidden.shape[1]
    model_width = hidden.shape[2]
    positions = lax.axis_index("ctx") * block_len + jnp.arange(block_len, dtype=jnp.int32)
    exponent = 2.0 * jnp.arange(HD // 2, dtype=F32) / HD
    inverse = jnp.power(10000.0, -exponent)
    angles = positions.astype(F32)[:, None] * inverse[None, :]
    cos, sin = jnp.cos(angles), jnp.sin(angles)
    cos = jnp.concatenate([cos, cos], axis=1)
    sin = jnp.concatenate([-sin, sin], axis=1)
    dma = pltpu.SemaphoreType.DMA
    return pl.pallas_call(
        kernel,
        out_shape=pltpu.VMEM(queries.shape, BF),
        in_specs=[
            pl.BlockSpec(memory_space=pl.ANY) for n in range(8)
        ],
        out_specs=pl.BlockSpec(memory_space=pltpu.VMEM),
        scratch_shapes=[
            pltpu.VMEM(kv_weight.shape, BF),
            pltpu.VMEM((1, model_width), F32),
            pltpu.VMEM((1, HD), F32),
            pltpu.VMEM((1, HD), F32),
            pltpu.VMEM((block_len, HD), F32),
            pltpu.VMEM((block_len, HD), F32),
            pltpu.VMEM((MEMBERS, 42, HD), BF),
            pltpu.VMEM((NZ, NX, NY, ROWS_A, HD), BF),
            pltpu.VMEM((NY, NZ, NX, ROWS_B, HD), BF),
            pltpu.VMEM((NX, NZ, NY, ROWS_C, HD), BF),
            pltpu.VMEM(hidden.shape, BF),
            pltpu.VMEM(queries.shape, BF),
            pltpu.VMEM((NZ, 2, 2 * block_len, PLANE_LANES), BF),
            pltpu.VMEM((4, 2, 2 * block_len, 256), F32),
            pltpu.VMEM((16, HD, 256), BF),
            pltpu.VMEM((24, HD, 256), BF),
            pltpu.VMEM(queries.shape, BF),
            pltpu.VMEM((16, HD, 256), BF),
            pltpu.VMEM((16, HD, 256), BF),
            dma((8,)), dma((8,)), dma((8,)), dma((12,)), dma((12,)), dma((4,)), dma((4,)),
            dma((20,)), dma((20,)), dma((20,)), dma((20,)),
            dma((64,)), dma((64,)), dma, dma,
            dma((16,)), dma((16,)), dma((16,)), dma((24,)), dma((8,)), dma((16,)), dma((16,)),
        ],
        compiler_params=pltpu.CompilerParams(
            collective_id=0, has_side_effects=True, vmem_limit_bytes=60 << 20
        ),
    )(
        kv_weight, hidden, queries, input_gain, query_gain, key_gain, cos, sin,
    )


def solution(mesh):
    return jax.shard_map(
        body,
        mesh=mesh,
        in_specs=(P("dp", "ctx", None), P("dp", "ctx", None), P(), P("ctx", None), P(), P()),
        out_specs=P("dp", "ctx", None),
        check_vma=False,
    )
```

```python
import jax
import jax.numpy as jnp
import numpy as np
from jax import lax
from jax.experimental import pallas as pl
from jax.experimental.pallas import tpu as pltpu
from jax.sharding import PartitionSpec as P

HD = 128
WINDOW = 1024
EPS = 1e-6
SCALE = 168.0 ** -0.5
NX, NY, NZ = 4, 4, 8
PLANE = NX * NY
SLABS = WINDOW // HD
MEMBERS = 8
ROWS_A, ROWS_B, ROWS_C = 80, 128, 128
PLANE_ROWS = 2 * (ROWS_A + ROWS_B + ROWS_C)
PLANE_LANES = 768
BF = jnp.bfloat16
F32 = jnp.float32
MESH = pl.DeviceIdType.MESH


def head_rotary(head, gain, cos, sin):
    mean = jnp.mean(head * head, axis=-1, keepdims=True)
    unit = head * lax.rsqrt(mean + EPS) * gain
    return unit * cos + pltpu.roll(unit, 64, 1) * sin


def kernel(
    w_hbm, h_hbm, q_hbm, gain_hbm, qg_hbm, kg_hbm, freq_hbm, o_ref,
    w_ref, gain_ref, qg_ref, kg_ref, freq_ref, landing, wa, wb, wc, h_ref, q_ref, xn, acc, kvs, kvb, qn, qb, ob,
    in_s, a_s, a_r, row_s, row_r, p_s, p_r, az_s, az_r, z_s, z_r, l_s, l_r, x_s, x_r,
    q_s, q_r, kv_s, kv_r, halo_s, o_s, o_r,
):
    c = lax.axis_index("dp")
    t = lax.axis_index("ctx")
    z = lax.div(t, PLANE)
    i = lax.rem(t, PLANE)
    y = lax.div(i, NX)
    x = lax.rem(i, NX)
    yh = lax.div(y, 2)
    yl = lax.rem(y, 2)
    block_len = h_ref.shape[1]

    def chip(zz, yy, xx):
        return zz * PLANE + yy * NX + xx

    def step(v, d, n):
        return lax.rem(v + (d % n), n)

    sibling = (1 - c, t)
    pending = []

    def remote(src, dst, send, recv, device):
        return pltpu.make_async_remote_copy(
            src_ref=src, dst_ref=dst, send_sem=send, recv_sem=recv,
            device_id=device, device_id_type=MESH,
        )

    def push(src, dst, send, recv, device):
        copy = remote(src, dst, send, recv, device)
        copy.start()
        pending.append(copy)

    def arrived(region, recv):
        pltpu.make_async_copy(region, region, recv).wait()

    loads = [
        pltpu.make_async_copy(src, dst, in_s.at[n])
        for n, (src, dst) in enumerate((
            (w_hbm, w_ref), (q_hbm, q_ref), (qg_hbm, qg_ref.at[0]), (kg_hbm, kg_ref.at[0]),
            (freq_hbm, freq_ref), (h_hbm, h_ref), (gain_hbm, gain_ref.at[0]),
        ))
    ]
    for load in loads:
        load.start()

    barrier = pltpu.get_barrier_semaphore()
    for r in range(1, 2 * PLANE):
        dev = (lax.rem(c + r % 2, 2), z * PLANE + lax.rem(i + r // 2, PLANE))
        pl.semaphore_signal(barrier, inc=1, device_id=dev, device_id_type=MESH)
    for d in (1, -1):
        pl.semaphore_signal(
            barrier, inc=1, device_id=(c, chip(step(z, d, NZ), y, x)), device_id_type=MESH
        )


    def query_heads(s):
        for h in range(16):
            head = q_ref[s, :, h * HD:(h + 1) * HD].astype(F32)
            qn[s, :, h * HD:(h + 1) * HD] = (head_rotary(head, qg, cos, sin) * SCALE).astype(BF)

    loads[4].wait()
    token = lax.broadcasted_iota(jnp.int32, (block_len, HD), 0) + t * block_len
    angle = token.astype(F32) * freq_ref[...]
    lane = lax.broadcasted_iota(jnp.int32, (block_len, HD), 1)
    cos = jnp.cos(angle)
    sin = jnp.where(lane < HD // 2, -jnp.sin(angle), jnp.sin(angle))
    loads[0].wait()
    pl.semaphore_wait(barrier, 2 * PLANE - 1 + 2)

    j = yl * NX + x
    for r in range(1, MEMBERS):
        peer = lax.rem(j + r, MEMBERS)
        pyl, px = lax.div(peer, NX), lax.rem(peer, NX)
        col = pl.multiple_of(pyl * 1024 + c * 512 + px * HD, HD)
        push(
            w_ref.at[:, pl.ds(col, HD)], landing.at[j], a_s.at[r], a_r.at[r],
            (c, chip(z, yh * 2 + pyl, px)),
        )
    col = pl.multiple_of(yl * 1024 + c * 512 + x * HD, HD)
    landing[j] = w_ref[:, pl.ds(col, HD)]

    def q_pieces(start):
        for k in range(8):
            for kk in range(2):
                low = lax.rem(i + k, 8)
                core = lax.rem(c + kk, 2)
                s = lax.div(low, 4)
                h = core * 4 + lax.rem(low, 4)
                src = qn.at[s, :, pl.ds(pl.multiple_of(h * 256, 256), 256)]
                dst = qb.at[i]
                dev = (core, z * PLANE + c * 8 + low)
                send, recv = q_s.at[k * 2 + kk], q_r.at[i]
                if k == 0 and kk == 0:
                    here = lax.div(i, 8) == c

                    @pl.when(here)
                    def _():
                        if start:
                            pltpu.make_async_copy(src, dst, recv).start()

                    @pl.when(jnp.logical_not(here))
                    def _():
                        copy = remote(src, dst, send, recv, dev)
                        copy.start() if start else copy.wait_send()
                else:
                    copy = remote(src, dst, send, recv, dev)
                    copy.start() if start else copy.wait_send()

    for load in loads[1:4]:
        load.wait()
    qg, kg = qg_ref[...], kg_ref[...]
    query_heads(0)
    for r in range(1, MEMBERS):
        arrived(landing.at[lax.rem(j + MEMBERS - r, MEMBERS)], a_r.at[r])
    rows = jnp.concatenate([landing[m].astype(F32) for m in range(MEMBERS)], axis=0).astype(BF)
    wa[z, x, y] = rows[:ROWS_A]
    wb[y, z, x] = rows[ROWS_A:ROWS_A + ROWS_B]
    wc[x, z, y] = rows[ROWS_A + ROWS_B:]

    for d in (1, 3, 2):
        push(wb.at[y, z, x], wb.at[y, z, x], row_s.at[d], row_r.at[d], (c, chip(z, y, step(x, d, NX))))
        push(wc.at[x, z, y], wc.at[x, z, y], row_s.at[4 + d], row_r.at[4 + d], (c, chip(z, step(y, d, NY), x)))
    for d in (1, 3, 2):
        push(wa.at[z, x, y], wa.at[z, x, y], row_s.at[8 + d], row_r.at[8 + d], (c, chip(z, step(y, d, NY), x)))
    query_heads(1)
    for d in (1, 3, 2):
        arrived(wb.at[y, z, step(x, -d, NX)], row_r.at[d])
        arrived(wc.at[x, z, step(y, -d, NY)], row_r.at[4 + d])

    def chunk(part, line, zz):
        return wb.at[line, zz] if part == 0 else wc.at[line, zz]

    def half(part, line, zz, which):
        ref = wb if part == 0 else wc
        return ref.at[line, zz, pl.ds(2 * which, 2)]

    def line_device(part, d):
        if part == 0:
            return (c, chip(z, step(y, d, NY), x))
        return (c, chip(z, y, step(x, d, NX)))

    own = (y, x)
    along = (NY, NX)

    def z_sem(part, way, d):
        return (part * 2 + way) * 5 + d

    def l_sem(part, way, kind, slot):
        return ((part * 2 + way) * 2 + kind) * 8 + slot

    def z_send(part, zz, way, d):
        dev = (c, chip(step(z, 1 if way == 0 else -1, NZ), y, x))
        ref = chunk(part, own[part], zz) if d < 4 else half(part, own[part], zz, way)
        n = z_sem(part, way, d)
        push(ref, ref, z_s.at[n], z_r.at[n], dev)

    def z_wait(part, zz, way, d):
        ref = chunk(part, own[part], zz) if d < 4 else half(part, own[part], zz, way)
        arrived(ref, z_r.at[z_sem(part, way, d)])

    def line_send(part, zz, slot):
        for way, d in ((0, 1), (1, -1)):
            ref = chunk(part, own[part], zz)
            n = l_sem(part, way, 0, slot)
            push(ref, ref, l_s.at[n], l_r.at[n], line_device(part, d))

    def line_relay(part, zz, slot):
        for way, d in ((0, 1), (1, -1)):
            line = step(own[part], -d, along[part])
            arrived(chunk(part, line, zz), l_r.at[l_sem(part, way, 0, slot)])
            ref = half(part, line, zz, way)
            n = l_sem(part, way, 1, slot)
            push(ref, ref, l_s.at[n], l_r.at[n], line_device(part, d))

    def line_finish(part, zz, slot):
        for way in range(2):
            line = step(own[part], 2, along[part])
            arrived(half(part, line, zz, way), l_r.at[l_sem(part, way, 1, slot)])

    def slots(k):
        if k == 0:
            return [(z, 0)]
        if k == 4:
            return [(step(z, 4, NZ), 7)]
        return [(step(z, -k, NZ), k), (step(z, k, NZ), 3 + k)]

    def norm_rows():
        def one(n, carry):
            at = pl.multiple_of(n * 16, 16)
            s, row = lax.div(at, block_len), pl.multiple_of(lax.rem(at, block_len), 16)
            v = h_ref[s, pl.ds(row, 16), :].astype(F32)
            mean = jnp.mean(v * v, axis=-1, keepdims=True)
            v = v * lax.rsqrt(mean + EPS) * gain_ref[...]
            pad = jnp.zeros((16, PLANE_LANES - PLANE_ROWS), F32)
            for zz in range(NZ):
                piece = jnp.concatenate([v[:, zz * PLANE_ROWS:(zz + 1) * PLANE_ROWS], pad], axis=1)
                xn[zz, c, pl.ds(at, 16), :] = piece.astype(BF)
            return carry

        lax.fori_loop(0, 2 * block_len // 16, one, 0)

    def plane_across():
        for d in (1, 3, 2):
            arrived(wa.at[z, x, step(y, -d, NY)], row_r.at[8 + d])
        for d in (1, 3, 2):
            push(wa.at[z, x], wa.at[z, x], p_s.at[d], p_r.at[d], (c, chip(z, y, step(x, d, NX))))

    def plane_send(zz, way, d):
        dev = (c, chip(step(z, 1 if way == 0 else -1, NZ), y, x))
        for which in range(2):
            if d < 4 or which == way:
                ref = wa.at[zz, pl.ds(2 * which, 2)]
                n = (way * 2 + which) * 5 + d
                push(ref, ref, az_s.at[n], az_r.at[n], dev)

    def plane_relay(k):
        if k == 0:
            for d in (1, 3, 2):
                arrived(wa.at[z, step(x, -d, NX)], p_r.at[d])
            plane_send(z, 0, 1)
            plane_send(z, 1, 1)
            return
        dev = [(c, chip(step(z, 1 if way == 0 else -1, NZ), y, x)) for way in range(2)]
        for which in range(2):
            for way in range(2):
                zz = step(z, -k if way == 0 else k, NZ)
                if k == 4 and which != way:
                    continue
                ref = wa.at[zz, pl.ds(2 * which, 2)]
                n = (way * 2 + which) * 5 + k
                arrived(ref, az_r.at[n])
                if k < 3 or (k == 3 and which == way):
                    push(ref, ref, az_s.at[n + 1], az_r.at[n + 1], dev[way])

    def rows_of(zz, nyl, nx):
        pieces = []
        for hi in range(2):
            ny = 2 * hi + nyl
            pieces.append(jnp.concatenate([wa[zz, nx, ny], wa[zz, nx + 1, ny]], axis=1))
            pieces.append(jnp.concatenate([wb[ny, zz, nx], wb[ny, zz, nx + 1]], axis=1))
            pieces.append(jnp.concatenate([wc[nx, zz, ny], wc[nx + 1, zz, ny]], axis=1))
        return jnp.concatenate(pieces, axis=0)

    def project(planes, first):
        def pair(n, carry):
            nyl, nx = lax.div(n, 2), 2 * lax.rem(n, 2)
            for g in range(2):
                term = None if first else acc[n, g]
                for zz in planes:
                    more = jnp.dot(
                        xn[zz, g, :, :PLANE_ROWS], rows_of(zz, nyl, nx), preferred_element_type=F32
                    )
                    term = more if term is None else term + more
                acc[n, g] = term
            return carry

        lax.fori_loop(0, 4, pair, 0)

    def complete(k):
        for zz, slot in slots(k):
            for part in range(2):
                line_finish(part, zz, slot)
        project([zz for zz, _ in slots(k)], k == 0)

    for k in range(5):
        if k > 0:
            for way, (zz, _) in enumerate(slots(k) if k < 4 else slots(k) * 2):
                for part in range(2):
                    z_wait(part, zz, way, k)
                    if k < 4:
                        z_send(part, zz, way, k + 1)
        else:
            for way in range(2):
                for part in range(2):
                    z_send(part, z, way, 1)
        for zz, slot in slots(k):
            for part in range(2):
                line_send(part, zz, slot)
        if k == 0:
            plane_across()
            q_pieces(True)
            for load in loads[5:]:
                load.wait()
            norm_rows()
            push(xn.at[:, c], xn.at[:, c], x_s, x_r, sibling)
        if k > 0:
            for zz, slot in slots(k - 1):
                for part in range(2):
                    line_relay(part, zz, slot)
            if k == 1:
                plane_relay(0)
            if k > 1:
                plane_relay(k - 1)
        if k == 3:
            arrived(xn.at[:, 1 - c], x_r)
        if k > 2:
            complete(k - 3)
    for zz, slot in slots(4):
        for part in range(2):
            line_relay(part, zz, slot)
    complete(2)
    complete(3)
    plane_relay(4)
    complete(4)

    def kv_pieces(start):
        for k in range(PLANE):
            u = lax.rem(i + k, PLANE)
            src, dst = kvs.at[u], kvb.at[SLABS + i]
            send, recv = kv_s.at[k], kv_r.at[SLABS + i]
            if k > 0:
                copy = remote(src, dst, send, recv, (c, z * PLANE + u))
                copy.start() if start else copy.wait_send()
            elif start:
                pltpu.make_async_copy(src, dst, recv).start()

    for g in range(2):
        for s in range(2):
            for h in range(4):
                rows, lanes = slice(s * block_len, (s + 1) * block_len), slice(h % 2 * HD, (h % 2 + 1) * HD)
                u = g * 8 + s * 4 + h
                kvs[u, :, :HD] = head_rotary(acc[h // 2, g, rows, lanes], kg, cos, sin).astype(BF)
                kvs[u, :, HD:] = acc[2 + h // 2, g, rows, lanes].astype(BF)
    kv_pieces(True)

    def halo(src):
        n = src - SLABS
        return remote(kvb.at[16 + n], kvb.at[n], halo_s.at[n], kv_r.at[n], (c, t + PLANE))

    def receive(k, carry):
        src = lax.rem(i + PLANE - k, PLANE)
        arrived(kvb.at[SLABS + src], kv_r.at[SLABS + src])

        @pl.when(jnp.logical_and(src >= SLABS, z < NZ - 1))
        def _():
            halo(src).start()

        return carry

    lax.fori_loop(0, PLANE, receive, 0)
    for n in range(PLANE):
        arrived(qb.at[n], q_r.at[n])

    unit_g = lax.div(i, 8)
    unit_s = lax.rem(lax.div(i, 4), 2)
    unit_h = c * 4 + lax.rem(i, 4)
    out_col = pl.multiple_of(unit_h * 256, 256)
    row_at = lax.broadcasted_iota(jnp.int32, (2 * HD, HD), 0)
    row_at = jnp.where(row_at >= HD, row_at - HD, row_at)
    col_at = lax.broadcasted_iota(jnp.int32, (2 * HD, HD), 1)

    def out_copy(slab):
        return remote(
            ob.at[slab], o_ref.at[unit_s, :, pl.ds(out_col, 256)],
            o_s.at[slab], o_r.at[unit_s * 8 + unit_h], (unit_g, z * PLANE + slab),
        )

    def attend(slab, first_half):
        q = jnp.concatenate([qb[slab, :, :HD], qb[slab, :, HD:]], axis=0)
        total = jnp.zeros((2 * HD, 1), F32)
        out = jnp.zeros((2 * HD, HD), F32)
        for b in range(9):
            keys = kvb[slab + b, :, :HD]
            values = kvb[slab + b, :, HD:]
            scores = lax.dot_general(q, keys, (((1,), (1,)), ((), ())), preferred_element_type=F32)
            weight = jnp.exp(scores)
            if b == 0:
                weight = jnp.where(col_at > row_at, weight, 0.0)
            if b == 8:
                weight = jnp.where(col_at <= row_at, weight, 0.0)
            elif first_half:
                seen = jnp.logical_or(z > 0, slab + b >= SLABS)
                weight = jnp.where(seen, weight, 0.0)
            total = total + jnp.sum(weight, axis=-1, keepdims=True)
            out = out + jnp.dot(weight.astype(BF), values, preferred_element_type=F32)
        out = (out / total).astype(BF)
        ob[slab] = jnp.concatenate([out[:HD], out[HD:]], axis=1)
        here = jnp.logical_and(unit_g == c, slab == i)

        @pl.when(here)
        def _():
            pltpu.make_async_copy(
                ob.at[slab], o_ref.at[unit_s, :, pl.ds(out_col, 256)], o_r.at[unit_s * 8 + unit_h]
            ).start()

        @pl.when(jnp.logical_not(here))
        def _():
            out_copy(slab).start()

    def late(n, carry):
        attend(8 + lax.rem(i + n, 8), False)
        return carry

    lax.fori_loop(0, 8, late, 0)

    for n in range(SLABS):
        @pl.when(z > 0)
        def _(n=n):
            arrived(kvb.at[n], kv_r.at[n])

        @pl.when(z == 0)
        def _(n=n):
            kvb[n] = jnp.zeros((HD, 2 * HD), BF)

    def early(n, carry):
        attend(lax.rem(i + n, 8), True)
        return carry

    lax.fori_loop(0, 8, early, 0)

    for s in range(2):
        for h in range(8):
            arrived(o_ref.at[s, :, pl.ds(h * 256, 256)], o_r.at[s * 8 + h])

    for copy in pending:
        copy.wait_send()
    q_pieces(False)
    kv_pieces(False)
    for n in range(SLABS):
        @pl.when(z < NZ - 1)
        def _(n=n):
            halo(SLABS + n).wait_send()
    for slab in range(PLANE):
        @pl.when(jnp.logical_not(jnp.logical_and(unit_g == c, slab == i)))
        def _(slab=slab):
            out_copy(slab).wait_send()


def body(hidden, queries, input_gain, kv_weight, query_gain, key_gain):
    block_len = hidden.shape[1]
    model_width = hidden.shape[2]
    inverse = 10000.0 ** (-2.0 * np.arange(HD // 2) / HD)
    freq = jnp.asarray(np.concatenate([inverse, inverse])[None, :].astype(np.float32))
    dma = pltpu.SemaphoreType.DMA
    return pl.pallas_call(
        kernel,
        out_shape=pltpu.VMEM(queries.shape, BF),
        in_specs=[
            pl.BlockSpec(memory_space=pl.ANY) for n in range(7)
        ],
        out_specs=pl.BlockSpec(memory_space=pltpu.VMEM),
        scratch_shapes=[
            pltpu.VMEM(kv_weight.shape, BF),
            pltpu.VMEM((1, model_width), F32),
            pltpu.VMEM((1, HD), F32),
            pltpu.VMEM((1, HD), F32),
            pltpu.VMEM((1, HD), F32),
            pltpu.VMEM((MEMBERS, 42, HD), BF),
            pltpu.VMEM((NZ, NX, NY, ROWS_A, HD), BF),
            pltpu.VMEM((NY, NZ, NX, ROWS_B, HD), BF),
            pltpu.VMEM((NX, NZ, NY, ROWS_C, HD), BF),
            pltpu.VMEM(hidden.shape, BF),
            pltpu.VMEM(queries.shape, BF),
            pltpu.VMEM((NZ, 2, 2 * block_len, PLANE_LANES), BF),
            pltpu.VMEM((4, 2, 2 * block_len, 256), F32),
            pltpu.VMEM((16, HD, 256), BF),
            pltpu.VMEM((24, HD, 256), BF),
            pltpu.VMEM(queries.shape, BF),
            pltpu.VMEM((16, HD, 256), BF),
            pltpu.VMEM((16, HD, 256), BF),
            dma((8,)), dma((8,)), dma((8,)), dma((12,)), dma((12,)), dma((4,)), dma((4,)),
            dma((20,)), dma((20,)), dma((20,)), dma((20,)),
            dma((64,)), dma((64,)), dma, dma,
            dma((16,)), dma((16,)), dma((16,)), dma((24,)), dma((8,)), dma((16,)), dma((16,)),
        ],
        compiler_params=pltpu.CompilerParams(
            collective_id=0, has_side_effects=True, vmem_limit_bytes=60 << 20
        ),
    )(
        kv_weight, hidden, queries, input_gain, query_gain, key_gain, freq,
    )


def solution(mesh):
    return jax.shard_map(
        body,
        mesh=mesh,
        in_specs=(P("dp", "ctx", None), P("dp", "ctx", None), P(), P("ctx", None), P(), P()),
        out_specs=P("dp", "ctx", None),
        check_vma=False,
    )
```
